256 devices in a mesh: dp: 32 (over x, z_lo, core), mp: 8 (over y, z_hi).
Axes of the slice: x: 4, y: 4, z: 8 (z_hi: 2, z_lo: 4; z = z_hi * 4 + z_lo), core: 2. Of those that a mesh axis runs over, the one named last changes fastest.
Arguments:
- gradients: bfloat16 [32, 59392, 128], P('dp', 'mp'), may hold values from -8 to 8
- weights: float32 [59392, 128], P('mp'), may hold values from -40 to 40
- first_moment: float32 [8, 7424, 128], P('mp', 'dp'), may hold values from -240 to 240
- second_moment: float32 [8, 7424, 128], P('mp', 'dp'), may hold values from 0.3 to 3
- owner_list: int32 [8, 7424], P('mp'), may hold values from 0 to 31, as said below
- norm_grads: bfloat16 [32, 2, 1024], P('dp'), may hold values from -6 to 6
- norm_state: float32 [3, 2, 1024], replicated, may hold values from -1.6 to 3, as said below
Outputs:
- new_weights: float32 [59392, 128], P('mp')
- new_first: float32 [8, 7424, 128], P('mp', 'dp')
- new_second: float32 [8, 7424, 128], P('mp', 'dp')
- new_norm_state: float32 [3, 2, 1024], replicated
- trust_ratios: float32 [7], replicated
The draws below stay inside these ranges and needn't reach their ends.
Inputs may be any that keep to these rules, and one draw needn't show every extreme that they name: `owner_list`: in every mp shard each dp index owns exactly 232 of the 7424 blocks. `norm_state`: gains near 1, second moments positive.
All inputs are finite; a program needn't handle non-finite values.
Results may differ from the reference program's by a relative error of at most 0.0003.
Values sent between devices are 32-bit elements; how exact they have to be, the bound alone decides.
A program may use at most 64 MiB of HBM per device.

```python
import math
import jax
import jax.numpy as jnp
from jax import lax

D = 1024
LANE = 128
QBLK = 1024
KBLK = 256
VBLK = 4096
NBLK = 7424
BPD = 232
N_DP = 32
N_MP = 8


def draw_gradients(key, part):
    shape = (N_DP, N_MP * NBLK, LANE)
    key_own = jax.random.fold_in(key, 0)
    own_part = jax.random.truncated_normal(key_own, -4.0, 4.0, shape, jnp.float32)
    return own_part.astype(jnp.bfloat16)


def draw_weights(key, part):
    shape = (N_MP * NBLK, LANE)
    key_value, key_rows, key_lanes = jax.random.split(key, 3)
    lane_scale = jnp.exp(jax.random.uniform(key_lanes, (1, LANE), jnp.float32, -0.6, 0.6))
    row_scale = jnp.exp(jax.random.uniform(key_rows, (shape[0], 1), jnp.float32, -1.15, 1.15))
    values = jax.random.truncated_normal(key_value, -4.0, 4.0, shape, jnp.float32)
    return values * row_scale * lane_scale


def draw_first_moment(key, part):
    shape = (N_MP, NBLK, LANE)
    owner_pos = (jnp.arange(NBLK, dtype=jnp.int32) // BPD).astype(jnp.float32) / max(N_DP - 1, 1)
    shard_pos = jnp.arange(N_MP, dtype=jnp.int32).astype(jnp.float32) / max(N_MP - 1, 1)
    rise = jnp.log(10.0)
    values = jax.random.truncated_normal(key, -4.0, 4.0, shape, jnp.float32)
    scale = jnp.exp(rise * owner_pos)[None, :, None] * jnp.exp(jnp.log(2.0) * shard_pos)[:, None, None]
    return values * scale


def draw_owner_list(key, part):
    shard_keys = jax.random.split(key, N_MP)
    shuffled = jax.vmap(lambda shard_key: jax.random.permutation(shard_key, NBLK))(shard_keys)
    return (shuffled // BPD).astype(jnp.int32)


def draw_norm_state(key, part):
    key_gain, key_first, key_second = jax.random.split(key, 3)
    gain_rows = 1.0 + 0.1 * jax.random.truncated_normal(key_gain, -4.0, 4.0, (2, D), jnp.float32)
    first_rows = 0.4 * jax.random.truncated_normal(key_first, -4.0, 4.0, (2, D), jnp.float32)
    second_rows = jnp.exp(jax.random.uniform(key_second, (2, D), jnp.float32, jnp.log(0.3), jnp.log(3.0)))
    return jnp.stack([gain_rows, first_rows, second_rows])


def block_scale(own_key, dims, cuts, smallest, top_value):
    def one(dim, blocks):
        heights = jax.random.uniform(jax.random.fold_in(jax.random.fold_in(own_key, 6), dim), (blocks,), jnp.float32, smallest / len(cuts), top_value / len(cuts))
        return jnp.repeat(jnp.exp(heights), dims[dim] // blocks).reshape((-1,) + (1,) * (len(dims) - dim - 1))

    loudness = one(*cuts[0])
    for cut in cuts[1:]:
        loudness = loudness * one(*cut)
    return loudness


def centred(own_key, dims, deviation, reach, cuts=(), held_as=jnp.bfloat16):
    gain = block_scale(own_key, dims, cuts, -0.22, 0.18) if cuts else 1.0
    entries = jax.random.normal(own_key, dims, jnp.float32) * deviation * gain
    return jnp.minimum(jnp.maximum(entries, -reach), reach).astype(held_as)


def setup_inputs(seed: int = 0) -> dict:
    streams_of = jax.random.split(jax.random.key(seed), 8)
    return {
        "gradients": draw_gradients(jax.random.fold_in(streams_of[7], 71), 0),
        "weights": draw_weights(jax.random.fold_in(streams_of[7], 71), 0),
        "first_moment": draw_first_moment(jax.random.fold_in(streams_of[7], 71), 0),
        "second_moment": jnp.clip(jnp.exp(math.log(3.0) - 2.3025851 * jax.random.uniform(streams_of[3], (N_MP, NBLK, LANE), jnp.float32) ** block_scale(streams_of[3], (N_MP, NBLK, LANE), ((0, 8), (1, 32)), -0.2, 0.2)), 0.3, 3.0),
        "owner_list": draw_owner_list(jax.random.fold_in(streams_of[7], 71), 0),
        "norm_grads": centred(streams_of[5], (N_DP, 2, D), 1.0, 6.0, ((0, 32),)),
        "norm_state": draw_norm_state(jax.random.fold_in(streams_of[7], 71), 0),
    }


beta_one = 0.9
beta_two = 0.99
bias_one = 1.0 - 0.9 ** 4
bias_two = 1.0 - 0.99 ** 4
epsilon = 1e-06
learning = 0.02
decay_rate = 0.01
matrices = 5

def block_matrix():
    position = jnp.arange(NBLK, dtype=jnp.int32)
    bounds = (QBLK, QBLK + KBLK, QBLK + KBLK + VBLK, 2 * QBLK + KBLK + VBLK)
    result = jnp.zeros((NBLK,), jnp.int32)
    for boundary in bounds:
        result = result + (position >= boundary).astype(jnp.int32)
    return result

def adam_step(gradient, moment_one, moment_two, weight):
    moment_one = beta_one * moment_one + (1.0 - beta_one) * gradient
    moment_two = beta_two * moment_two + (1.0 - beta_two) * gradient * gradient
    update = moment_one / bias_one / (jnp.sqrt(moment_two / bias_two) + epsilon) + decay_rate * weight
    return (moment_one, moment_two, update)

def member_table(matrix_of):
    return (matrix_of[:, None] == jnp.arange(matrices, dtype=jnp.int32)[None, :]).astype(jnp.float32)

def reference(gradients, weights, first_moment, second_moment, owner_list, norm_grads, norm_state):

    def add_replica(replica, running):
        return running + lax.dynamic_index_in_dim(gradients, replica, 0, keepdims=False).astype(jnp.float32)
    summed = lax.fori_loop(0, N_DP, add_replica, jnp.zeros(gradients.shape[1:], jnp.float32))
    matrix_of = block_matrix()
    stats = jnp.zeros((2, matrices), jnp.float32)
    pieces = []
    for shard_index in range(N_MP):
        owner_order = jnp.argsort(owner_list[shard_index], stable=True).astype(jnp.int32)
        gradient = summed[shard_index * NBLK:(shard_index + 1) * NBLK][owner_order]
        weight = weights[shard_index * NBLK:(shard_index + 1) * NBLK][owner_order]
        moment_one, moment_two, update = adam_step(gradient, first_moment[shard_index], second_moment[shard_index], weight)
        member = member_table(matrix_of[owner_order])
        squares = jnp.stack([lax.optimization_barrier(jnp.sum(weight * weight, axis=1)), lax.optimization_barrier(jnp.sum(update * update, axis=1))])
        stats = stats + jnp.dot(squares, member, precision=lax.Precision.HIGHEST)
        pieces.append((owner_order, weight, update, moment_one, moment_two, member))
    ratios = jnp.sqrt(stats[0]) / (jnp.sqrt(stats[1]) + epsilon)
    shards = []
    firsts = []
    seconds = []
    for owner_order, weight, update, moment_one, moment_two, member in pieces:
        row_rates = jnp.dot(member, ratios, precision=lax.Precision.HIGHEST)
        fresh_rows = weight - learning * row_rates[:, None] * update
        shards.append(jnp.zeros((NBLK, LANE), jnp.float32).at[owner_order].set(fresh_rows))
        firsts.append(moment_one)
        seconds.append(moment_two)
    norm_sum = lax.optimization_barrier(jnp.sum(norm_grads.astype(jnp.float32), axis=0))
    gain_rows = norm_state[0]
    norm_one, norm_two, norm_update = adam_step(norm_sum, norm_state[1], norm_state[2], gain_rows)
    norm_ratio = jnp.sqrt(lax.optimization_barrier(jnp.sum(gain_rows * gain_rows, axis=1))) / (jnp.sqrt(lax.optimization_barrier(jnp.sum(norm_update * norm_update, axis=1))) + epsilon)
    new_gains = gain_rows - learning * norm_ratio[:, None] * norm_update
    new_norm_state = jnp.stack([new_gains, norm_one, norm_two])
    trust_ratios = jnp.concatenate([ratios, norm_ratio])
    return (jnp.concatenate(shards, axis=0), jnp.stack(firsts), jnp.stack(seconds), new_norm_state, trust_ratios)
```

```python
import functools

import jax
import jax.numpy as jnp
from jax import lax
from jax.experimental import pallas as pl
from jax.experimental.pallas import tpu as pltpu
from jax.sharding import PartitionSpec as P

LANE = 128
NX, NZ, NC, ZH = 4, 4, 2, 2
QUERY, KEYS, VALUES = 1024, 256, 4096
MATRICES = 5
RBLK = 256
RPAD = 256

beta_one = 0.9
beta_two = 0.99
bias_one = 1.0 - 0.9**4
bias_two = 1.0 - 0.99**4
epsilon = 1e-06
learning = 0.02
decay_rate = 0.01

MESH = pl.DeviceIdType.MESH
VMEM = pltpu.VMEM
SMEM = pltpu.SMEM
f32 = jnp.float32
bf16 = jnp.bfloat16
i32 = jnp.int32


def matrix_bounds():
    return (QUERY, QUERY + KEYS, QUERY + KEYS + VALUES, 2 * QUERY + KEYS + VALUES)


def adam_step(gradient, moment_one, moment_two, weight):
    moment_one = beta_one * moment_one + (1.0 - beta_one) * gradient
    moment_two = beta_two * moment_two + (1.0 - beta_two) * gradient * gradient
    update = (
        moment_one / bias_one / (jnp.sqrt(moment_two / bias_two) + epsilon) + decay_rate * weight
    )
    return moment_one, moment_two, update


def tables_kernel(n, owner_ref, out_ref, own_s, m_s, t_s, a_s, b_s):
    rows = owner_ref.shape[0]
    owners = NX * NZ * NC
    own_s[...] = jnp.full((64, LANE), 99, i32)
    own_s[0:rows, :] = owner_ref[...]
    own = own_s[...]
    for o in range(owners):
        m_s[o * 64 : (o + 1) * 64, :] = jnp.where(own == o, 1.0, 0.0).astype(bf16)
    r0 = lax.broadcasted_iota(i32, (LANE, 2 * LANE), 0)
    c0 = lax.broadcasted_iota(i32, (LANE, 2 * LANE), 1)
    upper = jnp.where(r0 < c0, 1.0, 0.0).astype(bf16)
    prefix = jnp.dot(m_s[...], upper, preferred_element_type=f32)
    for o in range(owners):
        t_s[:, o * LANE : (o + 1) * LANE] = prefix[o * 64 : (o + 1) * 64, LANE:].astype(bf16)
    r1 = lax.broadcasted_iota(i32, (64, 64), 0)
    c1 = lax.broadcasted_iota(i32, (64, 64), 1)
    lower = jnp.where(c1 < r1, 1.0, 0.0).astype(bf16)
    above = jnp.dot(lower, t_s[...], preferred_element_type=f32)
    rank = jnp.zeros((64, LANE), f32)
    for o in range(owners):
        here = prefix[o * 64 : (o + 1) * 64, :LANE] + above[:, o * LANE : (o + 1) * LANE]
        rank = rank + jnp.where(own == o, here, 0.0)
    out_ref[0:64, :] = own * n + rank.astype(i32)
    rank_i = rank.astype(i32)
    sub = lax.broadcasted_iota(i32, (RPAD, LANE), 0)
    dev = lax.broadcasted_iota(i32, (owners, LANE), 0)
    lane = lax.broadcasted_iota(i32, (owners, LANE), 1).astype(f32)
    for i in range(rows):
        b_s[:, i * LANE : (i + 1) * LANE] = jnp.where(rank_i[i : i + 1, :] == sub, 1.0, 0.0).astype(bf16)
        mine = own[i : i + 1, :] == dev
        a_s[0:owners, i * LANE : (i + 1) * LANE] = jnp.where(mine, float(i), 0.0).astype(bf16)
        a_s[owners:, i * LANE : (i + 1) * LANE] = jnp.where(mine, lane, 0.0).astype(bf16)
    found = lax.dot_general(
        a_s[...], b_s[...], (((1,), (1,)), ((), ())), preferred_element_type=f32
    )
    order = (found[0:owners] * float(LANE) + found[owners:]).astype(i32)
    out_ref[64:96, :] = order[:, :LANE]
    out_ref[96:128, :] = order[:, LANE:]


def tables(owner, n):
    rows = owner.shape[0]
    return pl.pallas_call(
        functools.partial(tables_kernel, n),
        out_shape=jax.ShapeDtypeStruct((128, LANE), i32),
        in_specs=[pl.BlockSpec(memory_space=VMEM)],
        out_specs=pl.BlockSpec(memory_space=VMEM),
        scratch_shapes=[
            VMEM((64, LANE), i32),
            VMEM((NX * NZ * NC * 64, LANE), bf16),
            VMEM((64, NX * NZ * NC * LANE), bf16),
            VMEM((64, rows * LANE), bf16),
            VMEM((RPAD, rows * LANE), bf16),
        ],
        name="owner_tables",
    )(owner)


def order_at(tab, d, r):
    return tab[(64 + (r // LANE) * 32) * LANE + d * LANE + r % LANE]


def permute_kernel(n, tab, g_ref, w_ref, out_ref, wown_ref, idx_ref, gf):
    total = g_ref.shape[0]
    step = 256

    def widen(i, carry):
        at = pl.ds(pl.multiple_of(i * step, step), step)
        gf[at, :] = g_ref[at, :].astype(f32)
        return carry

    lax.fori_loop(0, total // step, widen, 0)

    def one(d, carry):
        for r in range(n):
            out_ref[d, pl.ds(r, 1), :] = gf[pl.ds(order_at(tab, d, r), 1), :]
        return carry

    lax.fori_loop(0, NX * NZ * NC, one, 0)
    me = lax.axis_index("dp")
    for r in range(n):
        b = order_at(tab, me, r)
        wown_ref[pl.ds(r, 1), :] = w_ref[pl.ds(b, 1), :]
        idx_ref[pl.ds(r, 1), :] = jnp.full((1, LANE), b, i32)


def permute(tab, grads, weights, n):
    total = grads.shape[0]
    return pl.pallas_call(
        functools.partial(permute_kernel, n),
        out_shape=(
            jax.ShapeDtypeStruct((NX * NZ * NC, n, LANE), f32),
            jax.ShapeDtypeStruct((n, LANE), f32),
            jax.ShapeDtypeStruct((n, LANE), i32),
        ),
        in_specs=[
            pl.BlockSpec(memory_space=SMEM),
            pl.BlockSpec(memory_space=VMEM),
            pl.BlockSpec(memory_space=VMEM),
        ],
        out_specs=(pl.BlockSpec(memory_space=VMEM),) * 3,
        scratch_shapes=[VMEM((total, LANE), f32)],
        name="permute_rows",
    )(tab, grads, weights)


def exchange_kernel(
    n, half, ny,
    gp, m1, m2, wown, idx, ng,
    dall, m1n, m2n, stats, nsum,
    rbuf, col, x2p, x2m, left, right, zbuf, tot,
    nb1, nb2, sb1, sb2, sb3,
    ps, pr, xs, xr, zs, zr,
    ns1, nr1, ns2, nr2, ss1, sr1, ss2, sr2, ss3, sr3,
    gzs, gzr, gxs, gxr, gps, gpr,
):
    me = lax.axis_index("dp")
    m = lax.axis_index("mp")
    x = me // (NZ * NC)
    z = (me // NC) % NZ
    c = me % NC
    y = m // ZH
    zh = m % ZH
    ha = pl.ds(0, half)
    hb = pl.ds(half, n - half)

    def at(x_, z_, c_):
        return x_ * (NZ * NC) + z_ * NC + c_

    xp, xm, xo = (x + 1) % NX, (x + 3) % NX, (x + 2) % NX
    up = (z // 2) * 2 - 1
    zk = [(z + up * (1 + k) + 8) % NZ for k in range(NZ)]
    oc = 1 - c
    xc = x * NC + c
    xcp = [(xc + j) % (NX * NC) for j in range(1, NX * NC)]

    def dev(d):
        return (d, m)

    partner = dev(at(x, z, oc))
    xc_dev = [dev(at(p // NC, z, p % NC)) for p in xcp]
    z_dev = [dev(at(x, (z + j) % NZ, c)) for j in range(1, NZ)]
    zz = zh * NZ + z
    zzp = [(zz + j) % (ZH * NZ) for j in range(1, ZH * NZ)]
    zz_dev = [(at(x, p % NZ, c), y * ZH + p // NZ) for p in zzp]
    yp = [(y + j) % ny for j in range(1, ny)]
    y_dev = [(me, p * ZH + zh) for p in yp]

    barrier = pltpu.get_barrier_semaphore()
    peers = xc_dev + zz_dev + y_dev
    for peer in peers:
        pl.semaphore_signal(barrier, inc=1, device_id=peer, device_id_type=MESH)
    nb1[xc] = ng[...].astype(f32)
    pl.semaphore_wait(barrier, len(peers))

    def send(src, dst, ssem, rsem, to):
        copy = pltpu.make_async_remote_copy(
            src_ref=src, dst_ref=dst, send_sem=ssem, recv_sem=rsem,
            device_id=to, device_id_type=MESH,
        )
        copy.start()
        return copy

    def arrived(dst, rsem):
        pltpu.make_async_copy(dst, dst, rsem).wait()

    started = []

    cols = (xo, xp, xm, x)
    for k in range(NZ):
        for j in range(4):
            started.append(
                send(gp.at[at(cols[j], zk[k], oc)], rbuf.at[j, k], ps.at[j, k], pr.at[j, k], partner)
            )
    for j in range(1, NX * NC):
        started.append(send(nb1.at[xc], nb1.at[xc], ns1.at[j], nr1.at[j], xc_dev[j - 1]))

    def pair_sum(j, k):
        arrived(rbuf.at[j, k], pr.at[j, k])
        return gp[at(cols[j], zk[k], c)] + rbuf[j, k]

    right_dev, left_dev = dev(at(xp, z, c)), dev(at(xm, z, c))

    def s1(k):
        col[0, k] = pair_sum(0, k)
        started.append(send(col.at[0, k, ha], x2p.at[k], xs.at[0, k], xr.at[0, k], right_dev))
        started.append(send(col.at[0, k, hb], x2m.at[k], xs.at[1, k], xr.at[1, k], left_dev))

    def s2(k):
        col[1, k] = pair_sum(1, k)
        started.append(send(col.at[1, k, hb], left.at[k, hb], xs.at[2, k], xr.at[2, k], right_dev))
        col[2, k] = pair_sum(2, k)
        started.append(send(col.at[2, k, ha], right.at[k, ha], xs.at[3, k], xr.at[3, k], left_dev))

    def s3(k):
        arrived(x2p.at[k], xr.at[0, k])
        col[1, k, ha] = col[1, k, ha] + x2p[k]
        started.append(send(col.at[1, k, ha], left.at[k, ha], xs.at[4, k], xr.at[4, k], right_dev))
        arrived(x2m.at[k], xr.at[1, k])
        col[2, k, hb] = col[2, k, hb] + x2m[k]
        started.append(send(col.at[2, k, hb], right.at[k, hb], xs.at[5, k], xr.at[5, k], left_dev))

    def s4(k):
        own = pair_sum(3, k)
        arrived(left.at[k, hb], xr.at[2, k])
        arrived(right.at[k, ha], xr.at[3, k])
        arrived(left.at[k, ha], xr.at[4, k])
        arrived(right.at[k, hb], xr.at[5, k])
        tot[k] = own + left[k] + right[k]
        if k < NZ - 1:
            started.append(
                send(tot.at[k], zbuf.at[z], zs.at[k], zr.at[z], dev(at(x, zk[k], c)))
            )

    s1(0)
    s2(0)
    s1(1)
    s3(0)
    s2(1)
    s1(2)
    s3(1)
    s4(0)
    s2(2)
    s1(3)
    s3(2)
    s4(1)
    s2(3)

    for j in range(1, NX * NC):
        p = (xc + NX * NC - j) % (NX * NC)
        arrived(nb1.at[p], nr1.at[j])
    run = nb1[0]
    for p in range(1, NX * NC):
        run = run + nb1[p]
    nb2[z] = run
    for j in range(1, NZ):
        started.append(send(nb2.at[z], nb2.at[z], ns2.at[j], nr2.at[j], z_dev[j - 1]))

    s3(3)
    s4(2)
    s4(3)
    gsum = tot[NZ - 1]
    for j in range(1, NZ):
        p = (z + j) % NZ
        arrived(zbuf.at[p], zr.at[p])
        gsum = gsum + zbuf[p]

    one, two, update = adam_step(gsum, m1[...], m2[...], wown[...])
    dall[me] = update

    zj = [z] + [(z + j) % NZ for j in range(1, NZ)]
    for j in range(1, NZ):
        started.append(send(dall.at[me], dall.at[me], gzs.at[j], gzr.at[j], z_dev[j - 1]))

    def spread(j):
        d = at(x, zj_here[j], c)
        if j > 0:
            arrived(dall.at[d], gzr.at[src_j[j]])
        started.append(send(dall.at[d], dall.at[d], gxs.at[0, j], gxr.at[0, j], right_dev))
        started.append(send(dall.at[d], dall.at[d], gxs.at[1, j], gxr.at[1, j], left_dev))
        started.append(send(dall.at[d], dall.at[d], gps.at[0, j], gpr.at[0, j], partner))

    zj_here = [z] + [(z + NZ - j) % NZ for j in range(1, NZ)]
    src_j = [0] + list(range(1, NZ))

    def forward(j):
        dl = at(xm, zj_here[j], c)
        arrived(dall.at[dl], gxr.at[0, j])
        started.append(send(dall.at[dl, ha], dall.at[dl, ha], gxs.at[2, j], gxr.at[2, j], right_dev))
        dr = at(xp, zj_here[j], c)
        arrived(dall.at[dr], gxr.at[1, j])
        started.append(send(dall.at[dr, hb], dall.at[dr, hb], gxs.at[3, j], gxr.at[3, j], left_dev))
        started.append(send(dall.at[dl], dall.at[dl], gps.at[1, j], gpr.at[1, j], partner))
        started.append(send(dall.at[dr], dall.at[dr], gps.at[2, j], gpr.at[2, j], partner))

    def opposite(j):
        do = at(xo, zj_here[j], c)
        arrived(dall.at[do, ha], gxr.at[2, j])
        arrived(dall.at[do, hb], gxr.at[3, j])
        started.append(send(dall.at[do], dall.at[do], gps.at[3, j], gpr.at[3, j], partner))

    spread(0)

    m1n[...] = one
    m2n[...] = two
    b = idx[...]
    bounds = (0,) + matrix_bounds() + (1 << 30,)
    wsq, usq = wown[...] * wown[...], update * update
    lane = lax.broadcasted_iota(i32, (8, LANE), 1)
    row = lax.broadcasted_iota(i32, (8, LANE), 0)
    tile = jnp.zeros((8, LANE), f32)
    for k in range(MATRICES):
        inside = (b >= bounds[k]) & (b < bounds[k + 1])
        ws = jnp.sum(jnp.where(inside, wsq, 0.0), keepdims=True)
        us = jnp.sum(jnp.where(inside, usq, 0.0), keepdims=True)
        tile = tile + jnp.where((lane == k) & (row == 0), ws, 0.0)
        tile = tile + jnp.where((lane == k) & (row == 1), us, 0.0)
    sb1[xc] = tile
    for j in range(1, NX * NC):
        started.append(send(sb1.at[xc], sb1.at[xc], ss1.at[j], sr1.at[j], xc_dev[j - 1]))

    spread(1)
    forward(0)
    spread(2)
    opposite(0)

    for j in range(1, NX * NC):
        arrived(sb1.at[(xc + NX * NC - j) % (NX * NC)], sr1.at[j])
    run = sb1[0]
    for p in range(1, NX * NC):
        run = run + sb1[p]
    sb2[y] = run
    for j in range(1, ny):
        started.append(send(sb2.at[y], sb2.at[y], ss2.at[j], sr2.at[j], y_dev[j - 1]))

    forward(1)
    spread(3)

    for j in range(1, ny):
        arrived(sb2.at[(y + ny - j) % ny], sr2.at[j])
    run = sb2[0]
    for p in range(1, ny):
        run = run + sb2[p]
    sb3[zz] = run
    for j in range(1, ZH * NZ):
        started.append(send(sb3.at[zz], sb3.at[zz], ss3.at[j], sr3.at[j], zz_dev[j - 1]))

    opposite(1)
    forward(2)
    opposite(2)
    forward(3)

    for j in range(1, NZ):
        arrived(nb2.at[(z + NZ - j) % NZ], nr2.at[j])
    run = nb2[0]
    for p in range(1, NZ):
        run = run + nb2[p]
    nsum[...] = run

    for j in range(1, ZH * NZ):
        arrived(sb3.at[(zz + ZH * NZ - j) % (ZH * NZ)], sr3.at[j])
    run = sb3[0]
    for p in range(1, ZH * NZ):
        run = run + sb3[p]
    stats[...] = run

    opposite(3)

    for j in range(NZ):
        for i, x_ in enumerate((x, xm, xp, xo)):
            arrived(dall.at[at(x_, zj_here[j], oc)], gpr.at[i, j])
    for copy in started:
        copy.wait_send()


def exchange(gp, m1, m2, wown, idx, ng, ny):
    n = gp.shape[1]
    half = (n // 2 + 7) // 8 * 8
    d = ng.shape[1]
    DMA = pltpu.SemaphoreType.DMA
    chunk = (n, LANE)
    return pl.pallas_call(
        functools.partial(exchange_kernel, n, half, ny),
        out_shape=(
            jax.ShapeDtypeStruct((NX * NZ * NC, n, LANE), f32),
            jax.ShapeDtypeStruct(chunk, f32),
            jax.ShapeDtypeStruct(chunk, f32),
            jax.ShapeDtypeStruct((8, LANE), f32),
            jax.ShapeDtypeStruct((2, d), f32),
        ),
        in_specs=[pl.BlockSpec(memory_space=VMEM)] * 6,
        out_specs=(pl.BlockSpec(memory_space=VMEM),) * 5,
        scratch_shapes=[
            VMEM((4, NZ) + chunk, f32),
            VMEM((3, NZ) + chunk, f32),
            VMEM((NZ, half, LANE), f32),
            VMEM((NZ, n - half, LANE), f32),
            VMEM((NZ,) + chunk, f32),
            VMEM((NZ,) + chunk, f32),
            VMEM((NZ,) + chunk, f32),
            VMEM((NZ,) + chunk, f32),
            VMEM((NX * NC, 2, d), f32),
            VMEM((NZ, 2, d), f32),
            VMEM((NX * NC, 8, LANE), f32),
            VMEM((ny, 8, LANE), f32),
            VMEM((ZH * NZ, 8, LANE), f32),
            DMA((4, NZ)), DMA((4, NZ)),
            DMA((6, NZ)), DMA((6, NZ)),
            DMA((NZ,)), DMA((NZ,)),
            DMA((NX * NC,)), DMA((NX * NC,)),
            DMA((NZ,)), DMA((NZ,)),
            DMA((NX * NC,)), DMA((NX * NC,)),
            DMA((4,)), DMA((4,)),
            DMA((ZH * NZ,)), DMA((ZH * NZ,)),
            DMA((NZ,)), DMA((NZ,)),
            DMA((4, NZ)), DMA((4, NZ)),
            DMA((4, NZ)), DMA((4, NZ)),
        ],
        compiler_params=pltpu.CompilerParams(collective_id=0, has_side_effects=True),
        name="exchange",
    )(gp, m1, m2, wown, idx, ng)


def apply_kernel(tab, dirs, w_ref, stats, nsum, nstate, out_ref, ns_ref, trust, rows):
    step = pl.program_id(0)
    wsq = stats[0:1, :]
    usq = stats[1:2, :]
    ratio = jnp.sqrt(wsq) / (jnp.sqrt(usq) + epsilon)
    lane = lax.broadcasted_iota(i32, (1, LANE), 1)

    @pl.when(step == 0)
    def _():
        for k in range(MATRICES):
            trust[k] = jnp.sum(jnp.where(lane == k, ratio, 0.0))
        gains = nstate[0]
        one, two, update = adam_step(nsum[...], nstate[1], nstate[2], gains)
        norm_ratio = jnp.sqrt(jnp.sum(gains * gains, axis=1, keepdims=True)) / (
            jnp.sqrt(jnp.sum(update * update, axis=1, keepdims=True)) + epsilon
        )
        ns_ref[0] = gains - learning * norm_ratio * update
        ns_ref[1] = one
        ns_ref[2] = two
        which = lax.broadcasted_iota(i32, (2, 1), 0)
        for k in range(2):
            trust[MATRICES + k] = jnp.sum(jnp.where(which == k, norm_ratio, 0.0))

    base = step * RBLK
    k = jnp.int32(0)
    for bound in matrix_bounds():
        k = k + (base >= bound).astype(i32)
    rate = learning * jnp.sum(jnp.where(lane == k, ratio, 0.0), axis=1, keepdims=True)
    for r in range(RBLK):
        rows[pl.ds(r, 1), :] = dirs[pl.ds(tab[base + r], 1), :]
    out_ref[...] = w_ref[...] - rate * rows[...]


def apply(tab, dirs, weights, stats, nsum, nstate):
    total = weights.shape[0]
    whole = pl.BlockSpec(memory_space=VMEM)
    block = pl.BlockSpec((RBLK, LANE), lambda i: (i, 0))
    return pl.pallas_call(
        apply_kernel,
        out_shape=(
            jax.ShapeDtypeStruct(weights.shape, f32),
            jax.ShapeDtypeStruct(nstate.shape, f32),
            jax.ShapeDtypeStruct((MATRICES + 2,), f32),
        ),
        grid=(total // RBLK,),
        in_specs=[pl.BlockSpec(memory_space=SMEM), whole, block, whole, whole, whole],
        out_specs=(block, whole, pl.BlockSpec(memory_space=SMEM)),
        scratch_shapes=[VMEM((RBLK, LANE), f32)],
        name="new_weights",
    )(tab, dirs, weights, stats, nsum, nstate)


def local(ny, gradients, weights, first_moment, second_moment, owner_list, norm_grads, norm_state):
    total = weights.shape[0]
    n = total // (NX * NZ * NC)
    tab = tables(owner_list.reshape(total // LANE, LANE), n).reshape(-1)
    gp, wown, idx = permute(tab, gradients[0], weights, n)
    dall, m1n, m2n, stats, nsum = exchange(
        gp, first_moment[0], second_moment[0], wown, idx, norm_grads[0], ny
    )
    new_weights, new_state, trust = apply(
        tab, dall.reshape(total, LANE), weights, stats, nsum, norm_state
    )
    return new_weights, m1n[None], m2n[None], new_state, trust


def solution(mesh):
    in_specs = (
        P("dp", "mp", None),
        P("mp", None),
        P("mp", "dp", None),
        P("mp", "dp", None),
        P("mp", None),
        P("dp", None, None),
        P(),
    )
    out_specs = (P("mp", None), P("mp", "dp", None), P("mp", "dp", None), P(), P())
    return jax.shard_map(
        functools.partial(local, mesh.shape["mp"] // ZH),
        mesh=mesh, in_specs=in_specs, out_specs=out_specs, check_vma=False,
    )
```

```python
import functools

import jax
import jax.numpy as jnp
from jax import lax
from jax.experimental import pallas as pl
from jax.experimental.pallas import tpu as pltpu
from jax.sharding import PartitionSpec as P

LANE = 128
NX, NZ, NC, ZH = 4, 4, 2, 2
QUERY, KEYS, VALUES = 1024, 256, 4096
MATRICES = 5
RBLK = 256
RPAD = 256
ORDER = 64 * LANE

beta_one = 0.9
beta_two = 0.99
bias_one = 1.0 - 0.9**4
bias_two = 1.0 - 0.99**4
epsilon = 1e-06
learning = 0.02
decay_rate = 0.01

MESH = pl.DeviceIdType.MESH
VMEM = pltpu.VMEM
SMEM = pltpu.SMEM
f32 = jnp.float32
bf16 = jnp.bfloat16
i32 = jnp.int32


def matrix_bounds():
    return (QUERY, QUERY + KEYS, QUERY + KEYS + VALUES, 2 * QUERY + KEYS + VALUES)


def adam_step(gradient, moment_one, moment_two, weight):
    moment_one = beta_one * moment_one + (1.0 - beta_one) * gradient
    moment_two = beta_two * moment_two + (1.0 - beta_two) * gradient * gradient
    update = (
        moment_one / bias_one / (jnp.sqrt(moment_two / bias_two) + epsilon) + decay_rate * weight
    )
    return moment_one, moment_two, update


def tables_kernel(n, owner_ref, out_ref, own_s, m_s, t_s, a_s, b_s):
    rows = owner_ref.shape[1] // LANE
    owners = NX * NZ * NC
    own_s[...] = jnp.full((64, LANE), 99, i32)
    for i in range(rows):
        own_s[i : i + 1, :] = owner_ref[:, i * LANE : (i + 1) * LANE]
    own = own_s[...]
    for o in range(owners):
        m_s[o * 64 : (o + 1) * 64, :] = jnp.where(own == o, 1.0, 0.0).astype(bf16)
    r0 = lax.broadcasted_iota(i32, (LANE, 2 * LANE), 0)
    c0 = lax.broadcasted_iota(i32, (LANE, 2 * LANE), 1)
    upper = jnp.where(r0 < c0, 1.0, 0.0).astype(bf16)
    prefix = jnp.dot(m_s[...], upper, preferred_element_type=f32)
    for o in range(owners):
        t_s[:, o * LANE : (o + 1) * LANE] = prefix[o * 64 : (o + 1) * 64, LANE:].astype(bf16)
    r1 = lax.broadcasted_iota(i32, (64, 64), 0)
    c1 = lax.broadcasted_iota(i32, (64, 64), 1)
    lower = jnp.where(c1 < r1, 1.0, 0.0).astype(bf16)
    above = jnp.dot(lower, t_s[...], preferred_element_type=f32)
    rank = jnp.zeros((64, LANE), f32)
    for o in range(owners):
        here = prefix[o * 64 : (o + 1) * 64, :LANE] + above[:, o * LANE : (o + 1) * LANE]
        rank = rank + jnp.where(own == o, here, 0.0)
    out_ref[0:64, :] = own * n + rank.astype(i32)
    rank_i = rank.astype(i32)
    sub = lax.broadcasted_iota(i32, (RPAD, LANE), 0)
    dev = lax.broadcasted_iota(i32, (owners, LANE), 0)
    lane = lax.broadcasted_iota(i32, (owners, LANE), 1).astype(f32)
    for i in range(rows):
        b_s[:, i * LANE : (i + 1) * LANE] = jnp.where(rank_i[i : i + 1, :] == sub, 1.0, 0.0).astype(bf16)
        mine = own[i : i + 1, :] == dev
        a_s[0:owners, i * LANE : (i + 1) * LANE] = jnp.where(mine, float(i), 0.0).astype(bf16)
        a_s[owners:, i * LANE : (i + 1) * LANE] = jnp.where(mine, lane, 0.0).astype(bf16)
    found = lax.dot_general(
        a_s[...], b_s[...], (((1,), (1,)), ((), ())), preferred_element_type=f32
    )
    order = (found[0:owners] * float(LANE) + found[owners:]).astype(i32)
    out_ref[pl.ds(64, owners, stride=2), :] = order[:, :LANE]
    out_ref[pl.ds(65, owners, stride=2), :] = order[:, LANE:]


def tables(owner, n):
    rows = owner.shape[1] // LANE
    return pl.pallas_call(
        functools.partial(tables_kernel, n),
        out_shape=jax.ShapeDtypeStruct((128, LANE), i32),
        in_specs=[pl.BlockSpec(memory_space=VMEM)],
        out_specs=pl.BlockSpec(memory_space=VMEM),
        scratch_shapes=[
            VMEM((64, LANE), i32),
            VMEM((NX * NZ * NC * 64, LANE), bf16),
            VMEM((64, NX * NZ * NC * LANE), bf16),
            VMEM((64, rows * LANE), bf16),
            VMEM((RPAD, rows * LANE), bf16),
        ],
        name="owner_tables",
    )(owner)


def exchange_kernel(
    n, half, ny,
    tab, g, w_hbm, m1, m2, ng,
    dall, m1n, m2n, stats, nsum,
    gf, wbuf, wown, idx,
    pbuf, rbuf, col, x2p, x2m, left, right, zrec, tot,
    nb1, nb2, sb1, sb2, sb3,
    ps, pr, xs, xr, zs, zr,
    ns1, nr1, ns2, nr2, ss1, sr1, ss2, sr2, ss3, sr3,
    gzs, gzr, gxs, gxr, gps, gpr, wsem,
):
    me = lax.axis_index("dp")
    m = lax.axis_index("mp")
    x = me // (NZ * NC)
    z = (me // NC) % NZ
    c = me % NC
    y = m // ZH
    zh = m % ZH
    ha = pl.ds(0, half)
    hb = pl.ds(half, n - half)

    def at(x_, z_, c_):
        return x_ * (NZ * NC) + z_ * NC + c_

    xp, xm, xo = (x + 1) % NX, (x + 3) % NX, (x + 2) % NX
    upper = z // 2
    inner = z + upper * (NZ - 1 - 2 * z)

    def mirror(v):
        return v + upper * (NZ - 1 - 2 * v)

    near = [z, mirror(1 - inner), mirror(2), mirror(3)]
    zk = near[::-1]
    away = 1 - 2 * upper
    z_step = [away, away, away * (1 - 2 * inner)]
    z_low = [(1 - v) // 2 for v in z_step]
    oc = 1 - c
    xc = x * NC + c
    xcp = [(xc + j) % (NX * NC) for j in range(1, NX * NC)]

    def dev(d):
        return (d, m)

    partner = dev(at(x, z, oc))
    xc_dev = [dev(at(p // NC, z, p % NC)) for p in xcp]
    z_dev = [dev(at(x, (z + j) % NZ, c)) for j in range(1, NZ)]
    zz = zh * NZ + z
    zzp = [(zz + j) % (ZH * NZ) for j in range(1, ZH * NZ)]
    zz_dev = [(at(x, p % NZ, c), y * ZH + p // NZ) for p in zzp]
    yp = [(y + j) % ny for j in range(1, ny)]
    y_dev = [(me, p * ZH + zh) for p in yp]

    weights_in = pltpu.make_async_copy(w_hbm, wbuf, wsem)
    weights_in.start()
    barrier = pltpu.get_barrier_semaphore()
    peers = xc_dev + zz_dev + y_dev
    for peer in peers:
        pl.semaphore_signal(barrier, inc=1, device_id=peer, device_id_type=MESH)
    nb1[xc] = ng[...].astype(f32)

    def widen(i, carry):
        rows = pl.ds(pl.multiple_of(i * 256, 256), 256)
        gf[rows, :] = g[rows, :].astype(f32)
        return carry

    lax.fori_loop(0, g.shape[0] // 256, widen, 0)
    unroll = n // 4

    def gather(d, dst):
        base = ORDER + d * RPAD

        def body(i, carry):
            for r in range(unroll):
                row = i * unroll + r
                dst[pl.ds(row, 1), :] = gf[pl.ds(tab[base + row], 1), :]
            return carry

        lax.fori_loop(0, n // unroll, body, 0)

    cols = (xo, xp, xm, x)

    def mine(j, k):
        return col.at[j, k] if j < 3 else tot.at[k]

    def collect(j, k):
        gather(at(cols[j], zk[k], oc), pbuf.at[j, k])
        gather(at(cols[j], zk[k], c), mine(j, k))

    for j in range(4):
        collect(j, 0)
    pl.semaphore_wait(barrier, len(peers))

    def send(src, dst, ssem, rsem, to):
        copy = pltpu.make_async_remote_copy(
            src_ref=src, dst_ref=dst, send_sem=ssem, recv_sem=rsem,
            device_id=to, device_id_type=MESH,
        )
        copy.start()
        return copy

    def arrived(dst, rsem):
        pltpu.make_async_copy(dst, dst, rsem).wait()

    started = []

    def give(j, k):
        started.append(send(pbuf.at[j, k], rbuf.at[j, k], ps.at[j, k], pr.at[j, k], partner))

    for j in range(4):
        give(j, 0)
    for j in range(1, NX * NC):
        started.append(send(nb1.at[xc], nb1.at[xc], ns1.at[j], nr1.at[j], xc_dev[j - 1]))

    def pair_sum(j, k):
        arrived(rbuf.at[j, k], pr.at[j, k])
        return mine(j, k)[...] + rbuf[j, k]

    right_dev, left_dev = dev(at(xp, z, c)), dev(at(xm, z, c))

    def s1(k):
        col[0, k] = pair_sum(0, k)
        started.append(send(col.at[0, k, ha], x2p.at[k], xs.at[0, k], xr.at[0, k], right_dev))
        started.append(send(col.at[0, k, hb], x2m.at[k], xs.at[1, k], xr.at[1, k], left_dev))

    def s2(k):
        col[1, k] = pair_sum(1, k)
        started.append(send(col.at[1, k, hb], left.at[k, hb], xs.at[2, k], xr.at[2, k], right_dev))
        col[2, k] = pair_sum(2, k)
        started.append(send(col.at[2, k, ha], right.at[k, ha], xs.at[3, k], xr.at[3, k], left_dev))

    def s3(k):
        arrived(x2p.at[k], xr.at[0, k])
        col[1, k, ha] = col[1, k, ha] + x2p[k]
        started.append(send(col.at[1, k, ha], left.at[k, ha], xs.at[4, k], xr.at[4, k], right_dev))
        arrived(x2m.at[k], xr.at[1, k])
        col[2, k, hb] = col[2, k, hb] + x2m[k]
        started.append(send(col.at[2, k, hb], right.at[k, hb], xs.at[5, k], xr.at[5, k], left_dev))

    def s4(k):
        own = pair_sum(3, k)
        arrived(left.at[k, hb], xr.at[2, k])
        arrived(right.at[k, ha], xr.at[3, k])
        arrived(left.at[k, ha], xr.at[4, k])
        arrived(right.at[k, hb], xr.at[5, k])
        tot[k] = own + left[k] + right[k]
        if k < NZ - 1:
            pl.when(inner == 0)(functools.partial(z_send, k))

    def z_send(k):
        send(
            tot.at[k], zrec.at[z_low[k], zk[k]], zs.at[k], zr.at[z_low[k], zk[k]],
            dev(at(x, z + z_step[k], c)),
        )

    def z_chain(k):
        @pl.when(inner == 1)
        def _():
            arrived(zrec.at[z_low[k], zk[k]], zr.at[z_low[k], zk[k]])
            tot[k] = tot[k] + zrec[z_low[k], zk[k]]
            z_send(k)

    def more(k, js):
        for j in js:
            collect(j, k)
            give(j, k)

    more(1, (0, 1))
    s1(0)
    s2(0)
    more(1, (2, 3))
    s1(1)
    s3(0)
    more(2, (0, 1))
    s2(1)
    more(2, (2, 3))
    s1(2)
    s3(1)
    s4(0)
    more(3, (0, 1))
    s2(2)
    more(3, (2, 3))
    s1(3)
    s3(2)
    s4(1)
    z_chain(0)
    s2(3)

    for j in range(1, NX * NC):
        p = (xc + NX * NC - j) % (NX * NC)
        arrived(nb1.at[p], nr1.at[j])
    run = nb1[0]
    for p in range(1, NX * NC):
        run = run + nb1[p]
    nb2[z] = run
    for j in range(1, NZ):
        started.append(send(nb2.at[z], nb2.at[z], ns2.at[j], nr2.at[j], z_dev[j - 1]))

    s3(3)
    s4(2)
    z_chain(1)

    weights_in.wait()
    base = ORDER + me * RPAD

    def own_rows(i, carry):
        for r in range(unroll):
            row = i * unroll + r
            b = tab[base + row]
            wown[pl.ds(row, 1), :] = wbuf[pl.ds(b, 1), :]
            idx[pl.ds(row, 1), :] = jnp.full((1, LANE), b, i32)
        return carry

    lax.fori_loop(0, n // unroll, own_rows, 0)
    s4(3)
    z_chain(2)

    @pl.when(z > 0)
    def _():
        arrived(zrec.at[0, z], zr.at[0, z])
        tot[NZ - 1] = tot[NZ - 1] + zrec[0, z]

    @pl.when(z < NZ - 1)
    def _():
        arrived(zrec.at[1, z], zr.at[1, z])
        tot[NZ - 1] = tot[NZ - 1] + zrec[1, z]

    gsum = tot[NZ - 1]

    one, two, update = adam_step(gsum, m1[...], m2[...], wown[...])
    dall[me] = update

    def z_pass(d, z_, sem, step):
        send(dall.at[d], dall.at[d], gzs.at[sem], gzr.at[z_], dev(at(x, z + step, c)))

    pl.when(z < NZ - 1)(functools.partial(z_pass, me, z, 0, 1))
    pl.when(z > 0)(functools.partial(z_pass, me, z, 1, -1))

    def spread(j):
        d = at(x, near[j], c)
        if j > 0:
            arrived(dall.at[d], gzr.at[near[j]])
            pl.when(inner == 1)(
                functools.partial(z_pass, d, near[j], 1 + j, away if j == 1 else -away)
            )
        started.append(send(dall.at[d], dall.at[d], gxs.at[0, j], gxr.at[0, j], right_dev))
        started.append(send(dall.at[d], dall.at[d], gxs.at[1, j], gxr.at[1, j], left_dev))
        started.append(send(dall.at[d], dall.at[d], gps.at[0, j], gpr.at[0, j], partner))

    def forward(j):
        dl = at(xm, near[j], c)
        arrived(dall.at[dl], gxr.at[0, j])
        started.append(send(dall.at[dl, ha], dall.at[dl, ha], gxs.at[2, j], gxr.at[2, j], right_dev))
        dr = at(xp, near[j], c)
        arrived(dall.at[dr], gxr.at[1, j])
        started.append(send(dall.at[dr, hb], dall.at[dr, hb], gxs.at[3, j], gxr.at[3, j], left_dev))
        started.append(send(dall.at[dl], dall.at[dl], gps.at[1, j], gpr.at[1, j], partner))
        started.append(send(dall.at[dr], dall.at[dr], gps.at[2, j], gpr.at[2, j], partner))

    def opposite(j):
        do = at(xo, near[j], c)
        arrived(dall.at[do, ha], gxr.at[2, j])
        arrived(dall.at[do, hb], gxr.at[3, j])
        started.append(send(dall.at[do], dall.at[do], gps.at[3, j], gpr.at[3, j], partner))

    spread(0)

    m1n[...] = one
    m2n[...] = two
    b = idx[...]
    bounds = (0,) + matrix_bounds() + (1 << 30,)
    wsq, usq = wown[...] * wown[...], update * update
    lane = lax.broadcasted_iota(i32, (8, LANE), 1)
    row = lax.broadcasted_iota(i32, (8, LANE), 0)
    tile = jnp.zeros((8, LANE), f32)
    for k in range(MATRICES):
        inside = (b >= bounds[k]) & (b < bounds[k + 1])
        ws = jnp.sum(jnp.where(inside, wsq, 0.0), keepdims=True)
        us = jnp.sum(jnp.where(inside, usq, 0.0), keepdims=True)
        tile = tile + jnp.where((lane == k) & (row == 0), ws, 0.0)
        tile = tile + jnp.where((lane == k) & (row == 1), us, 0.0)
    sb1[xc] = tile
    for j in range(1, NX * NC):
        started.append(send(sb1.at[xc], sb1.at[xc], ss1.at[j], sr1.at[j], xc_dev[j - 1]))

    spread(1)
    forward(0)
    spread(2)
    opposite(0)

    for j in range(1, NX * NC):
        arrived(sb1.at[(xc + NX * NC - j) % (NX * NC)], sr1.at[j])
    run = sb1[0]
    for p in range(1, NX * NC):
        run = run + sb1[p]
    sb2[y] = run
    for j in range(1, ny):
        started.append(send(sb2.at[y], sb2.at[y], ss2.at[j], sr2.at[j], y_dev[j - 1]))

    forward(1)
    spread(3)

    for j in range(1, ny):
        arrived(sb2.at[(y + ny - j) % ny], sr2.at[j])
    run = sb2[0]
    for p in range(1, ny):
        run = run + sb2[p]
    sb3[zz] = run
    for j in range(1, ZH * NZ):
        started.append(send(sb3.at[zz], sb3.at[zz], ss3.at[j], sr3.at[j], zz_dev[j - 1]))

    opposite(1)
    forward(2)
    opposite(2)
    forward(3)

    for j in range(1, NZ):
        arrived(nb2.at[(z + NZ - j) % NZ], nr2.at[j])
    run = nb2[0]
    for p in range(1, NZ):
        run = run + nb2[p]
    nsum[...] = run

    for j in range(1, ZH * NZ):
        arrived(sb3.at[(zz + ZH * NZ - j) % (ZH * NZ)], sr3.at[j])
    run = sb3[0]
    for p in range(1, ZH * NZ):
        run = run + sb3[p]
    stats[...] = run

    opposite(3)

    for j in range(NZ):
        for i, x_ in enumerate((x, xm, xp, xo)):
            arrived(dall.at[at(x_, near[j], oc)], gpr.at[i, j])
    for copy in started:
        copy.wait_send()
    for k in range(NZ - 1):
        arrived(tot.at[k], zs.at[k])
    pl.when(z < NZ - 1)(lambda: arrived(dall.at[me], gzs.at[0]))
    pl.when(z > 0)(lambda: arrived(dall.at[me], gzs.at[1]))

    @pl.when(inner == 1)
    def _():
        for j in range(1, NZ):
            arrived(dall.at[me], gzs.at[1 + j])


def exchange(tab, grads, weights, m1, m2, ng, ny):
    n = m1.shape[0]
    half = (n // 2 + 7) // 8 * 8
    total = grads.shape[0]
    d = ng.shape[1]
    DMA = pltpu.SemaphoreType.DMA
    chunk = (n, LANE)
    whole = pl.BlockSpec(memory_space=VMEM)
    return pl.pallas_call(
        functools.partial(exchange_kernel, n, half, ny),
        out_shape=(
            jax.ShapeDtypeStruct((NX * NZ * NC, n, LANE), f32),
            jax.ShapeDtypeStruct(chunk, f32),
            jax.ShapeDtypeStruct(chunk, f32),
            jax.ShapeDtypeStruct((8, LANE), f32),
            jax.ShapeDtypeStruct((2, d), f32),
        ),
        in_specs=[
            pl.BlockSpec(memory_space=SMEM), whole, pl.BlockSpec(memory_space=pl.ANY),
            whole, whole, whole,
        ],
        out_specs=(whole,) * 5,
        scratch_shapes=[
            VMEM((total, LANE), f32),
            VMEM((total, LANE), f32),
            VMEM(chunk, f32),
            VMEM(chunk, i32),
            VMEM((4, NZ) + chunk, f32),
            VMEM((4, NZ) + chunk, f32),
            VMEM((3, NZ) + chunk, f32),
            VMEM((NZ, half, LANE), f32),
            VMEM((NZ, n - half, LANE), f32),
            VMEM((NZ,) + chunk, f32),
            VMEM((NZ,) + chunk, f32),
            VMEM((2, NZ) + chunk, f32),
            VMEM((NZ,) + chunk, f32),
            VMEM((NX * NC, 2, d), f32),
            VMEM((NZ, 2, d), f32),
            VMEM((NX * NC, 8, LANE), f32),
            VMEM((ny, 8, LANE), f32),
            VMEM((ZH * NZ, 8, LANE), f32),
            DMA((4, NZ)), DMA((4, NZ)),
            DMA((6, NZ)), DMA((6, NZ)),
            DMA((NZ,)), DMA((2, NZ)),
            DMA((NX * NC,)), DMA((NX * NC,)),
            DMA((NZ,)), DMA((NZ,)),
            DMA((NX * NC,)), DMA((NX * NC,)),
            DMA((4,)), DMA((4,)),
            DMA((ZH * NZ,)), DMA((ZH * NZ,)),
            DMA((NZ + 1,)), DMA((NZ,)),
            DMA((4, NZ)), DMA((4, NZ)),
            DMA((4, NZ)), DMA((4, NZ)),
            DMA(()),
        ],
        compiler_params=pltpu.CompilerParams(
            collective_id=0, has_side_effects=True, vmem_limit_bytes=36 * 2**20
        ),
        name="exchange",
    )(tab, grads, weights, m1, m2, ng)


def apply_kernel(
    tab, dirs, w_hbm, stats, nsum, nstate, m1, m2,
    out_hbm, ns_ref, trust, m1n, m2n,
    wbuf, obuf, wsem, osem,
):
    blocks = w_hbm.shape[0] // RBLK

    def block(ref, i):
        return ref.at[pl.ds(pl.multiple_of(i * RBLK, RBLK), RBLK)]

    def load(i):
        return pltpu.make_async_copy(block(w_hbm, i), block(wbuf, i), wsem.at[i])

    def save(i):
        return pltpu.make_async_copy(block(obuf, i), block(out_hbm, i), osem.at[i])

    lax.fori_loop(0, blocks, lambda i, carry: (load(i).start(), carry)[1], 0)

    wsq = stats[0:1, :]
    usq = stats[1:2, :]
    ratio = jnp.sqrt(wsq) / (jnp.sqrt(usq) + epsilon)
    lane = lax.broadcasted_iota(i32, (1, LANE), 1)

    def weigh(i, carry):
        base = i * RBLK
        for r in range(RBLK):
            obuf[pl.ds(base + r, 1), :] = dirs[pl.ds(tab[base + r], 1), :]
        k = jnp.int32(0)
        for bound in matrix_bounds():
            k = k + (base >= bound).astype(i32)
        rate = learning * jnp.sum(jnp.where(lane == k, ratio, 0.0), axis=1, keepdims=True)
        load(i).wait()
        at = pl.ds(pl.multiple_of(base, RBLK), RBLK)
        obuf[at, :] = wbuf[at, :] - rate * obuf[at, :]
        save(i).start()
        return carry

    lax.fori_loop(0, blocks, weigh, 0)

    m1n[...] = m1[...]
    m2n[...] = m2[...]
    for k in range(MATRICES):
        trust[k] = jnp.sum(jnp.where(lane == k, ratio, 0.0))
    gains = nstate[0]
    one, two, update = adam_step(nsum[...], nstate[1], nstate[2], gains)
    norm_ratio = jnp.sqrt(jnp.sum(gains * gains, axis=1, keepdims=True)) / (
        jnp.sqrt(jnp.sum(update * update, axis=1, keepdims=True)) + epsilon
    )
    ns_ref[0] = gains - learning * norm_ratio * update
    ns_ref[1] = one
    ns_ref[2] = two
    which = lax.broadcasted_iota(i32, (2, 1), 0)
    for k in range(2):
        trust[MATRICES + k] = jnp.sum(jnp.where(which == k, norm_ratio, 0.0))

    lax.fori_loop(0, blocks, lambda i, carry: (save(i).wait(), carry)[1], 0)


def apply(tab, dirs, weights, stats, nsum, nstate, m1, m2):
    total = weights.shape[0]
    whole = pl.BlockSpec(memory_space=VMEM)
    scalars = pl.BlockSpec(memory_space=SMEM)
    place = pl.BlockSpec(memory_space=pl.ANY)
    return pl.pallas_call(
        apply_kernel,
        out_shape=(
            jax.ShapeDtypeStruct(weights.shape, f32),
            jax.ShapeDtypeStruct(nstate.shape, f32),
            jax.ShapeDtypeStruct((MATRICES + 2,), f32),
            jax.ShapeDtypeStruct(m1.shape, f32),
            jax.ShapeDtypeStruct(m2.shape, f32),
        ),
        in_specs=[scalars, whole, place, whole, whole, whole, whole, whole],
        out_specs=(place, whole, scalars, whole, whole),
        scratch_shapes=[
            VMEM((total, LANE), f32),
            VMEM((total, LANE), f32),
            pltpu.SemaphoreType.DMA((total // RBLK,)),
            pltpu.SemaphoreType.DMA((total // RBLK,)),
        ],
        compiler_params=pltpu.CompilerParams(vmem_limit_bytes=20 * 2**20),
        name="new_weights",
    )(tab, dirs, weights, stats, nsum, nstate, m1, m2)


def local(ny, gradients, weights, first_moment, second_moment, owner_list, norm_grads, norm_state):
    total = weights.shape[0]
    n = total // (NX * NZ * NC)
    tab = tables(owner_list, n).reshape(-1)
    dall, m1n, m2n, stats, nsum = exchange(
        tab, gradients[0], weights, first_moment[0], second_moment[0], norm_grads[0], ny
    )
    new_weights, new_state, trust, m1n, m2n = apply(
        tab, dall.reshape(total, LANE), weights, stats, nsum, norm_state, m1n, m2n
    )
    return new_weights, m1n[None], m2n[None], new_state, trust


def solution(mesh):
    in_specs = (
        P("dp", "mp", None),
        P("mp", None),
        P("mp", "dp", None),
        P("mp", "dp", None),
        P("mp", None),
        P("dp", None, None),
        P(),
    )
    out_specs = (P("mp", None), P("mp", "dp", None), P("mp", "dp", None), P(), P())
    return jax.shard_map(
        functools.partial(local, mesh.shape["mp"] // ZH),
        mesh=mesh, in_specs=in_specs, out_specs=out_specs, check_vma=False,
    )
```
